32 devices in a mesh: groups: 2 (over x), mp: 8 (over z, y), psg: 2 (over core).
Axes of the slice: x: 2, y: 2, z: 4, core: 2. Of those that a mesh axis runs over, the one named last changes fastest.
Arguments:
- tokens: bfloat16 [512, 1024], P(('groups', 'mp', 'psg')), parts along dimension 0, may hold values from -6 to 6
- enc_gain: float32 [1024], replicated, may hold values from 0.25 to 1.75
- w_in: bfloat16 [1024, 32768], P(None, 'mp'), may hold values from -0.1875 to 0.1875
- w_out: bfloat16 [32768, 1024], P('mp'), may hold values from -0.046875 to 0.046875
- final_gain: float32 [1024], replicated, may hold values from 0.25 to 1.75
- w_keyval: bfloat16 [1024, 2, 16384], P(None, None, 'mp'), may hold values from -0.1875 to 0.1875
- answer_states: bfloat16 [256, 1024], P('groups'), parts along dimension 0, may hold values from -6 to 6
- dec_gain: float32 [1024], replicated, may hold values from 0.25 to 1.75
- w_query: bfloat16 [1024, 16384], P(None, 'mp')
- w_attn_out: bfloat16 [16384, 1024], P('mp'), may hold values from -0.046875 to 0.046875
- passage_lengths: int32 [32], P('groups'), parts along dimension 0, may hold values from 1 to 16
- passage_owner: int32 [32], P('groups'), parts along dimension 0, may hold values from 0 to 3, as said below
- answer_lengths: int32 [8], P('groups'), parts along dimension 0, may hold values from 1 to 64, 128 in all
Outputs:
- encoded: bfloat16 [512, 1024], P(('groups', 'mp', 'psg')), parts along dimension 0
- answer: bfloat16 [256, 1024], P(('groups', 'mp')), parts along dimension 0
The draws below stay inside these ranges and needn't reach their ends.
There are 2 independent parts, one for each index of `groups`. The reference program is written for one: setup_inputs(seed, part) draws one part's arguments, and reference() takes and returns one part's arrays. A program takes and returns all parts, laid end to end along the dimension named above; an argument that names none is the same for every part. Nothing has to cross between parts.
Inputs may be any that keep to these rules, and one draw needn't show every extreme that they name: `passage_owner`: every one of the 4 questions owns at least one passage.
All inputs are finite; a program needn't handle non-finite values.
Results may differ from the reference program's by a relative error of at most 0.028.
Values may be sent and summed in bfloat16 or wider, within the bound.
A program may use at most 128 MiB of HBM per device.

```python
import math
import jax
import jax.numpy as jnp
import numpy as np
from jax import lax

D = 1024
FF = 32768
HEADS = 128
DH = 128
P_SLOT = 16
NQ = 4
ANS = 128
INNER = 16384
TOKENS = 256
NPASS = 16


def draw_w_query(key, part):
    base_key = jax.random.fold_in(jax.random.fold_in(key, 11), 0)
    base = jax.random.normal(base_key, (D, INNER), jnp.float32)
    return (base * D ** (-0.5)).astype(jnp.bfloat16)


def draw_passage_owner(key, part):
    count = TOKENS // P_SLOT
    owner_key, order_key = jax.random.split(jax.random.fold_in(key, 7))
    owners = jax.random.randint(owner_key, (count,), 0, NQ, dtype=jnp.int32)
    order = jax.random.permutation(order_key, count)
    owners = owners.at[order[:NQ]].set(jnp.arange(NQ, dtype=jnp.int32))
    return owners


def touch_ends(drawn, stream_key, smallest, top_value):
    index_at = [jax.random.randint(jax.random.fold_in(stream_key, axis), (), 0, length) for axis, length in enumerate(drawn.shape)]
    longest = drawn.shape.index(max(drawn.shape))
    next_to = index_at[:longest] + [(index_at[longest] + 1) % drawn.shape[longest]] + index_at[longest + 1:]
    return drawn.at[tuple(index_at)].set(smallest).at[tuple(next_to)].set(top_value)


def shard_levels(key, extent, cuts, low, largest):
    def one(axis_at, shards_of):
        draws = jax.random.uniform(jax.random.fold_in(jax.random.fold_in(key, 6), axis_at), (shards_of,), jnp.float32, low / len(cuts), largest / len(cuts))
        return jnp.repeat(jnp.exp(draws), extent[axis_at] // shards_of).reshape((-1,) + (1,) * (len(extent) - axis_at - 1))

    level = one(*cuts[0])
    for cut in cuts[1:]:
        level = level * one(*cut)
    return level


def split_up(count, total, most, skew):
    loads = [(1 << 20) // math.isqrt(standing ** skew) + 1 for standing in range(2, count + 1)]
    rest, given = total - most - (count - 1), [1] * (count - 1)
    while rest > 0:
        free = [i for i in range(count - 1) if given[i] < most]
        pool, remaining = sum([loads[i] for i in free]), rest
        for i in free:
            more = min(most - given[i], max(1, remaining * loads[i] // pool), rest)
            given[i] = given[i] + more
            rest = rest - more
    return np.array([most] + given)


def ragged(own_key, count, total, most, slope):
    if count == 2:
        one = jax.random.randint(own_key, (), max(1, total - most), min(most, total - 1) + 1)
        return jnp.stack([one, total - one])
    lengths = jnp.asarray(split_up(count, total, most, slope), jnp.int32)
    couples = (count - 1) // 2
    donor, taker = lengths[1:1 + 2 * couples:2], lengths[2:2 + 2 * couples:2]
    slack = jnp.minimum(donor - 1, most - taker)
    passed = jax.random.randint(jax.random.fold_in(own_key, 1), (couples,), 0, 1 << 20) % (slack + 1)
    lengths = lengths.at[1:1 + 2 * couples:2].set(donor - passed).at[2:2 + 2 * couples:2].set(taker + passed)
    return lengths[jax.random.permutation(jax.random.fold_in(own_key, 2), count)]


def bell_draw(key, shape, width, limit, shards=(), held_as=jnp.bfloat16):
    drawn = width * jax.random.normal(key, shape, jnp.float32)
    if shards:
        drawn = drawn * shard_levels(key, shape, shards, -0.22, 0.18)
    return jnp.clip(drawn, -limit, limit).astype(held_as)


def setup_inputs(seed: int = 0, part: int = 0) -> dict:
    key_list = jax.random.split(jax.random.key(seed), 14)
    own_keys = jax.random.split(jax.random.fold_in(key_list[13], part), 14)
    tokens = bell_draw(own_keys[0], (TOKENS, D), 1.0, 6.0, ((0, 16),))
    enc_gain = jnp.clip(1.0 + 0.15 * jax.random.normal(key_list[1], (D,), jnp.float32), 0.25, 1.75)
    w_in = bell_draw(key_list[2], (D, FF), D ** -0.5, 0.1875, ((1, 8),))
    w_out = bell_draw(key_list[3], (FF, D), (FF // 2) ** -0.5, 0.046875, ((0, 8),))
    final_gain = jnp.clip(1.0 + 0.15 * jax.random.normal(key_list[4], (D,), jnp.float32), 0.25, 1.75)
    w_keyval = bell_draw(key_list[5], (D, 2, INNER), D ** -0.5, 0.1875, ((2, 8),))
    answer_states = bell_draw(own_keys[6], (ANS, D), 1.0, 6.0)
    dec_gain = jnp.clip(1.0 + 0.15 * jax.random.normal(key_list[7], (D,), jnp.float32), 0.25, 1.75)
    w_query = draw_w_query(jax.random.fold_in(key_list[13], 71), part)
    w_attn_out = bell_draw(key_list[9], (INNER, D), INNER ** -0.5, 0.046875, ((0, 8),))
    passage_lengths = touch_ends(jax.random.randint(own_keys[10], (NPASS,), 1, P_SLOT + 1), jax.random.fold_in(own_keys[10], 1), 1, P_SLOT).astype(jnp.int32)
    passage_owner = draw_passage_owner(jax.random.fold_in(jax.random.fold_in(key_list[13], part), 71), part)
    answer_lengths = ragged(own_keys[12], NQ, ANS, ANS // 2, 1).astype(jnp.int32)
    return dict(tokens=tokens, enc_gain=enc_gain, w_in=w_in, w_out=w_out, final_gain=final_gain, w_keyval=w_keyval, answer_states=answer_states, dec_gain=dec_gain, w_query=w_query, w_attn_out=w_attn_out, passage_lengths=passage_lengths, passage_owner=passage_owner, answer_lengths=answer_lengths)


eps = 1e-06

def norm_rows(states, gain):
    wide = states.astype(jnp.float32)
    factor = lax.rsqrt(lax.optimization_barrier(jnp.mean(wide * wide, axis=-1, keepdims=True)) + eps)
    return wide * factor * gain

def key_mask(token_index, passage_lengths, passage_owner, answer_lengths, answer_count):
    passage = token_index // P_SLOT
    place = token_index % P_SLOT
    count = passage_lengths.shape[0]
    match = passage[:, None] == jnp.arange(count, dtype=jnp.int32)[None, :]
    token_length = lax.optimization_barrier(jnp.sum(jnp.where(match, passage_lengths[None, :], 0), axis=1))
    token_owner = lax.optimization_barrier(jnp.sum(jnp.where(match, passage_owner[None, :], 0), axis=1))
    ends = jnp.cumsum(answer_lengths).astype(jnp.int32)
    answer_index = jnp.arange(answer_count, dtype=jnp.int32)
    question = lax.optimization_barrier(jnp.sum((answer_index[:, None] >= ends[None, :]).astype(jnp.int32), axis=1))
    return (place < token_length)[None, :] & (token_owner[None, :] == question[:, None])

def reference(tokens, enc_gain, w_in, w_out, final_gain, w_keyval, answer_states, dec_gain, w_query, w_attn_out, passage_lengths, passage_owner, answer_lengths):
    normed = norm_rows(tokens, enc_gain).astype(jnp.bfloat16)
    blocks = normed.reshape(TOKENS // P_SLOT, P_SLOT, D)

    def feed(block):
        hidden = jnp.maximum(jnp.dot(block, w_in, preferred_element_type=jnp.float32), 0.0).astype(jnp.bfloat16)
        return jnp.dot(hidden, w_out, preferred_element_type=jnp.float32)
    ffn = lax.map(feed, blocks).reshape(TOKENS, D)
    encoded = (tokens.astype(jnp.float32) + ffn).astype(jnp.bfloat16)
    memory = norm_rows(encoded, final_gain).astype(jnp.bfloat16)
    joined = jnp.dot(memory, w_keyval.reshape(D, 2 * INNER), preferred_element_type=jnp.float32).astype(jnp.bfloat16)
    keys = joined[:, :INNER].reshape(TOKENS, HEADS, DH).transpose(1, 0, 2)
    values = joined[:, INNER:].reshape(TOKENS, HEADS, DH).transpose(1, 0, 2)
    normed_answer = norm_rows(answer_states, dec_gain).astype(jnp.bfloat16)
    query = jnp.dot(normed_answer, w_query, preferred_element_type=jnp.float32).astype(jnp.bfloat16)
    query = query.reshape(ANS, HEADS, DH).transpose(1, 0, 2)
    allowed = key_mask(jnp.arange(TOKENS, dtype=jnp.int32), passage_lengths, passage_owner, answer_lengths, ANS)

    def attend(operands):
        head_query, head_keys, head_values = operands
        scores = jnp.dot(head_query, head_keys.T, preferred_element_type=jnp.float32) * DH ** (-0.5)
        scores = jnp.where(allowed, scores, -1e+30)
        top = lax.optimization_barrier(jnp.max(scores, axis=1, keepdims=True))
        weights = jnp.where(allowed, jnp.exp(scores - top), 0.0)
        total = lax.optimization_barrier(jnp.sum(weights, axis=1, keepdims=True))
        summed = jnp.dot(weights.astype(jnp.bfloat16), head_values, preferred_element_type=jnp.float32)
        return (summed / total).astype(jnp.bfloat16)
    context = lax.map(attend, (query, keys, values)).transpose(1, 0, 2).reshape(ANS, INNER)
    answer = (answer_states.astype(jnp.float32) + jnp.dot(context, w_attn_out, preferred_element_type=jnp.float32)).astype(jnp.bfloat16)
    return (encoded, answer)
```

```python
import functools

import jax
import jax.numpy as jnp
from jax import lax
from jax.experimental import pallas as pl
from jax.experimental.pallas import tpu as pltpu
from jax.sharding import PartitionSpec as P

DH = 128
P_SLOT = 16
EPS = 1e-06
MESH = pl.DeviceIdType.MESH
F32 = jnp.float32
BF16 = jnp.bfloat16


def norm_rows(states, gain):
    wide = states.astype(F32)
    factor = lax.rsqrt(jnp.mean(wide * wide, axis=-1, keepdims=True) + EPS)
    return wide * factor * gain


def tile_of(width, most):
    tile = min(width, most)
    while width % tile:
        tile //= 2
    return tile


def kernel(
    n,
    cores,
    tokens_ref,
    enc_gain_ref,
    final_gain_ref,
    dec_gain_ref,
    answers_ref,
    own_answers_ref,
    lengths_ref,
    owner_ref,
    rows_ref,
    w_in_hbm,
    w_out_hbm,
    w_kv_hbm,
    w_query_hbm,
    w_proj_hbm,
    encoded_ref,
    answer_ref,
    w_in,
    w_out,
    w_kv,
    w_query,
    w_proj,
    normed_all,
    hidden,
    part,
    send1,
    recv1,
    memory_all,
    keys,
    values,
    query,
    context,
    part2,
    send2,
    recv2,
    final_all,
    load_sem,
    ag_send,
    ag_recv,
    rs_send,
    rs_recv,
    mem_send,
    mem_recv,
    fwd_send,
    fwd_recv,
    rs2_send,
    rs2_recv,
    fin_send,
    fin_recv,
):
    me = lax.axis_index("mp")
    core = lax.axis_index("psg")
    rows, width = tokens_ref.shape
    hidden_count = w_in.shape[1]
    inner = w_query.shape[1]
    answer_count = answers_ref.shape[0]
    out_count = answer_count // n
    chunks1, chunks2 = send1.shape[0], send2.shape[0]
    chunk1, chunk2 = send1.shape[-1], send2.shape[-1]

    first = pl.multiple_of(core * inner, inner)
    loads = [
        pltpu.make_async_copy(w_query_hbm.at[:, pl.ds(first, inner)], w_query, load_sem.at[0]),
        pltpu.make_async_copy(w_in_hbm, w_in, load_sem.at[1]),
        pltpu.make_async_copy(w_out_hbm, w_out, load_sem.at[2]),
        pltpu.make_async_copy(w_kv_hbm, w_kv, load_sem.at[3]),
        pltpu.make_async_copy(w_proj_hbm.at[pl.ds(first, inner), :], w_proj, load_sem.at[4]),
    ]
    for load in loads:
        load.start()

    barrier = pltpu.get_barrier_semaphore()
    peers = [lax.rem(me + k, n) for k in range(1, n)]
    others = [lax.rem(core + k, cores) for k in range(1, cores)]
    for peer in peers:
        pl.semaphore_signal(barrier, inc=1, device_id={"mp": peer}, device_id_type=MESH)
    for other in others:
        pl.semaphore_signal(barrier, inc=1, device_id={"psg": other}, device_id_type=MESH)
    normed_all[me] = norm_rows(tokens_ref[...], enc_gain_ref[...]).astype(BF16)
    pl.semaphore_wait(barrier, n - 1 + cores - 1)

    def to_peer(src, dst, send_sem, recv_sem, peer):
        return pltpu.make_async_remote_copy(
            src_ref=src, dst_ref=dst, send_sem=send_sem, recv_sem=recv_sem,
            device_id={"mp": peer}, device_id_type=MESH,
        )

    def to_core(src, dst, send_sem, recv_sem, other):
        return pltpu.make_async_remote_copy(
            src_ref=src, dst_ref=dst, send_sem=send_sem, recv_sem=recv_sem,
            device_id={"psg": other}, device_id_type=MESH,
        )

    def gather_copy(source, k, peer):
        return to_peer(normed_all.at[source], normed_all.at[source], ag_send.at[k], ag_recv.at[source], peer)

    for k, peer in enumerate(peers):
        gather_copy(me, k, peer).start()

    normed_answer = norm_rows(answers_ref[...], dec_gain_ref[...]).astype(BF16)
    loads[0].wait()
    q_tile = tile_of(inner, 512)

    def query_step(i, carry):
        at = pl.ds(pl.multiple_of(i * q_tile, q_tile), q_tile)
        query[:, at] = jnp.dot(normed_answer, w_query[:, at], preferred_element_type=F32).astype(BF16)
        return carry

    lax.fori_loop(0, inner // q_tile, query_step, 0)

    loads[1].wait()
    for k, peer in enumerate(peers):
        gather_copy(peer, k, peer).wait_recv()
    for k, peer in enumerate(peers):
        gather_copy(me, k, peer).wait_send()

    normed = normed_all[...].reshape(n * rows, width)
    h_tile = tile_of(hidden_count, 512)

    def hidden_step(i, carry):
        at = pl.ds(pl.multiple_of(i * h_tile, h_tile), h_tile)
        product = jnp.dot(normed, w_in[:, at], preferred_element_type=F32)
        hidden[:, at] = jnp.maximum(product, 0.0).astype(BF16)
        return carry

    lax.fori_loop(0, hidden_count // h_tile, hidden_step, 0)
    loads[2].wait()

    def sum_copy(c, source, k, peer):
        return to_peer(
            send1.at[c, peer], recv1.at[c, source], rs_send.at[c, k], rs_recv.at[c, source], peer
        )

    def out_step(c, carry):
        at = pl.ds(pl.multiple_of(c * chunk1, chunk1), chunk1)
        product = jnp.dot(hidden[...], w_out[:, at], preferred_element_type=F32)
        product = product.reshape(n, rows, chunk1)
        part[c] = product
        send1[c] = product.astype(BF16)
        for k, peer in enumerate(peers):
            sum_copy(c, me, k, peer).start()
        return carry

    lax.fori_loop(0, chunks1, out_step, 0)

    for c in range(chunks1):
        at = slice(c * chunk1, (c + 1) * chunk1)
        total = part[c, me]
        for k, peer in enumerate(peers):
            sum_copy(c, peer, k, peer).wait_recv()
            total = total + recv1[c, peer].astype(F32)
        encoded_ref[:, at] = (tokens_ref[:, at].astype(F32) + total).astype(BF16)
    memory_all[0, me] = norm_rows(encoded_ref[...], final_gain_ref[...]).astype(BF16)

    def memory_copy(source, k, peer):
        return to_peer(
            memory_all.at[0, source], memory_all.at[0, source], mem_send.at[k], mem_recv.at[source], peer
        )

    def forward_copy(source, s, other):
        return to_core(
            memory_all.at[0, source], memory_all.at[cores - s, source],
            fwd_send.at[s - 1, source], fwd_recv.at[cores - s - 1, source], other,
        )

    for k, peer in enumerate(peers):
        memory_copy(me, k, peer).start()
    for s, other in enumerate(others, 1):
        forward_copy(me, s, other).start()
    for c in range(chunks1):
        for k, peer in enumerate(peers):
            sum_copy(c, me, k, peer).wait_send()
    loads[3].wait()
    loads[4].wait()

    half = n * rows
    count = cores * half
    place_at = lax.broadcasted_iota(jnp.int32, (1, count), 1)
    slot = place_at // half
    block = (place_at % half) // rows
    token = (block * cores + (core + slot) % cores) * rows + place_at % rows
    passage = token // P_SLOT
    token_length = jnp.zeros((1, count), jnp.int32)
    token_owner = jnp.zeros((1, count), jnp.int32)
    for i in range(lengths_ref.shape[0]):
        token_length = jnp.where(passage == i, lengths_ref[i], token_length)
        token_owner = jnp.where(passage == i, owner_ref[i], token_owner)
    answer_at = lax.broadcasted_iota(jnp.int32, (answer_count, 1), 0)
    question = jnp.zeros((answer_count, 1), jnp.int32)
    end = jnp.int32(0)
    for i in range(rows_ref.shape[0]):
        end = end + rows_ref[i]
        question = question + jnp.where(answer_at >= end, 1, 0)
    token_key = jnp.where(token % P_SLOT < token_length, token_owner, -1)
    allowed = token_key == question

    for k, peer in enumerate(peers):
        memory_copy(peer, k, peer).wait_recv()
        for s, other in enumerate(others, 1):
            forward_copy(peer, s, other).start()

    k_tile = tile_of(inner, 512)

    def project(s):
        memory = memory_all[s].reshape(half, width)

        def step(i, carry):
            at = pl.ds(pl.multiple_of(i * k_tile, k_tile), k_tile)
            keys[s, :, at] = jnp.dot(memory, w_kv[0, :, at], preferred_element_type=F32).astype(BF16)
            values[s, :, at] = jnp.dot(memory, w_kv[1, :, at], preferred_element_type=F32).astype(BF16)
            return carry

        lax.fori_loop(0, inner // k_tile, step, 0)

    project(0)
    for s, other in enumerate(others, 1):
        for source in [me] + peers:
            pltpu.make_async_remote_copy(
                src_ref=memory_all.at[0, source], dst_ref=memory_all.at[s, source],
                send_sem=fwd_send.at[s - 1, source], recv_sem=fwd_recv.at[s - 1, source],
                device_id={"psg": other}, device_id_type=MESH,
            ).wait_recv()
        project(s)

    for h in range(inner // DH):
        at = slice(h * DH, (h + 1) * DH)
        head_keys = keys[:, :, at].reshape(count, DH)
        head_values = values[:, :, at].reshape(count, DH)
        scores = lax.dot_general(
            query[:, at], head_keys, (((1,), (1,)), ((), ())), preferred_element_type=F32
        ) * DH ** (-0.5)
        scores = jnp.where(allowed, scores, -1e30)
        top = jnp.max(scores, axis=1, keepdims=True)
        weights = jnp.where(allowed, jnp.exp(scores - top), 0.0)
        total = jnp.sum(weights, axis=1, keepdims=True)
        summed = jnp.dot(weights.astype(BF16), head_values, preferred_element_type=F32)
        context[:, at] = (summed / total).astype(BF16)

    def sum2_copy(c, source, k, peer):
        return to_peer(
            send2.at[c, peer], recv2.at[c, source], rs2_send.at[c, k], rs2_recv.at[c, source], peer
        )

    for c in range(chunks2):
        product = jnp.dot(
            context[...], w_proj[:, c * chunk2 : (c + 1) * chunk2], preferred_element_type=F32
        )
        for j in range(n):
            block_rows = product[j * out_count : (j + 1) * out_count]
            part2[c, j] = block_rows
            send2[c, j] = block_rows.astype(BF16)
        for k, peer in enumerate(peers):
            sum2_copy(c, me, k, peer).start()

    for k, peer in enumerate(peers):
        memory_copy(me, k, peer).wait_send()
    for s, other in enumerate(others, 1):
        for source in [me] + peers:
            forward_copy(source, s, other).wait_send()

    for c in range(chunks2):
        total = part2[c, me]
        for k, peer in enumerate(peers):
            sum2_copy(c, peer, k, peer).wait_recv()
            total = total + recv2[c, peer].astype(F32)
        final_all[0, :, c * chunk2 : (c + 1) * chunk2] = total

    def final_copy(s, other):
        return to_core(
            final_all.at[0], final_all.at[cores - s], fin_send.at[s - 1], fin_recv.at[cores - s - 1], other
        )

    for s, other in enumerate(others, 1):
        final_copy(s, other).start()
    for c in range(chunks2):
        for k, peer in enumerate(peers):
            sum2_copy(c, me, k, peer).wait_send()
    total = final_all[0]
    for s, other in enumerate(others, 1):
        pltpu.make_async_remote_copy(
            src_ref=final_all.at[0], dst_ref=final_all.at[s],
            send_sem=fin_send.at[s - 1], recv_sem=fin_recv.at[s - 1],
            device_id={"psg": other}, device_id_type=MESH,
        ).wait_recv()
        total = total + final_all[s]
    answer_ref[...] = (own_answers_ref[me].astype(F32) + total).astype(BF16)
    for s, other in enumerate(others, 1):
        final_copy(s, other).wait_send()


def per_device(
    n,
    cores,
    tokens,
    enc_gain,
    w_in,
    w_out,
    final_gain,
    w_keyval,
    answer_states,
    dec_gain,
    w_query,
    w_attn_out,
    passage_lengths,
    passage_owner,
    answer_lengths,
):
    rows, width = tokens.shape
    hidden_count = w_in.shape[1]
    inner = w_query.shape[1] // cores
    answer_count = answer_states.shape[0]
    out_count = answer_count // n
    half = n * rows
    chunk1 = tile_of(width, 256)
    chunk2 = tile_of(width, 512)
    chunks1, chunks2 = width // chunk1, width // chunk2
    core = lax.axis_index("psg")
    w_kv = lax.dynamic_slice_in_dim(w_keyval, core * inner, inner, 2).transpose(1, 0, 2)
    vmem = pl.BlockSpec(memory_space=pltpu.VMEM)
    smem = pl.BlockSpec(memory_space=pltpu.SMEM)
    hbm = pl.BlockSpec(memory_space=pl.ANY)
    dma = pltpu.SemaphoreType.DMA
    others = max(cores - 1, 1)
    return pl.pallas_call(
        functools.partial(kernel, n, cores),
        out_shape=(
            jax.ShapeDtypeStruct((rows, width), BF16),
            jax.ShapeDtypeStruct((out_count, width), BF16),
        ),
        in_specs=[vmem] * 6 + [smem] * 3 + [hbm] * 5,
        out_specs=(vmem, vmem),
        scratch_shapes=[
            pltpu.VMEM((width, hidden_count), BF16),
            pltpu.VMEM((hidden_count, width), BF16),
            pltpu.VMEM((2, width, inner), BF16),
            pltpu.VMEM((width, inner), BF16),
            pltpu.VMEM((inner, width), BF16),
            pltpu.VMEM((n, rows, width), BF16),
            pltpu.VMEM((half, hidden_count), BF16),
            pltpu.VMEM((chunks1, n, rows, chunk1), F32),
            pltpu.VMEM((chunks1, n, rows, chunk1), BF16),
            pltpu.VMEM((chunks1, n, rows, chunk1), BF16),
            pltpu.VMEM((cores, n, rows, width), BF16),
            pltpu.VMEM((cores, half, inner), BF16),
            pltpu.VMEM((cores, half, inner), BF16),
            pltpu.VMEM((answer_count, inner), BF16),
            pltpu.VMEM((answer_count, inner), BF16),
            pltpu.VMEM((chunks2, n, out_count, chunk2), F32),
            pltpu.VMEM((chunks2, n, out_count, chunk2), BF16),
            pltpu.VMEM((chunks2, n, out_count, chunk2), BF16),
            pltpu.VMEM((cores, out_count, width), F32),
            dma((5,)),
            dma((n,)),
            dma((n,)),
            dma((chunks1, n)),
            dma((chunks1, n)),
            dma((n,)),
            dma((n,)),
            dma((others, n)),
            dma((others, n)),
            dma((chunks2, n)),
            dma((chunks2, n)),
            dma((others,)),
            dma((others,)),
        ],
        compiler_params=pltpu.CompilerParams(
            collective_id=0, has_side_effects=True, vmem_limit_bytes=58 * 1024 * 1024
        ),
    )(
        tokens,
        enc_gain.reshape(1, width),
        final_gain.reshape(1, width),
        dec_gain.reshape(1, width),
        answer_states,
        answer_states.reshape(n, out_count, width),
        passage_lengths,
        passage_owner,
        answer_lengths,
        w_in,
        w_out,
        w_kv,
        w_query,
        w_attn_out,
    )


def solution(mesh):
    placed = (
        P(("groups", "mp", "psg"), None),
        P(),
        P(None, "mp"),
        P("mp", None),
        P(),
        P(None, None, "mp"),
        P("groups", None),
        P(),
        P(None, "mp"),
        P("mp", None),
        P("groups"),
        P("groups"),
        P("groups"),
    )
    return jax.shard_map(
        functools.partial(per_device, mesh.shape["mp"], mesh.shape["psg"]),
        mesh=mesh,
        in_specs=placed,
        out_specs=(P(("groups", "mp", "psg"), None), P(("groups", "mp"), None)),
        check_vma=False,
    )
```

```python
import functools

import jax
import jax.numpy as jnp
from jax import lax
from jax.experimental import pallas as pl
from jax.experimental.pallas import tpu as pltpu
from jax.sharding import PartitionSpec as P

DH = 128
P_SLOT = 16
EPS = 1e-06
MESH = pl.DeviceIdType.MESH
F32 = jnp.float32
BF16 = jnp.bfloat16


def norm_rows(states, gain):
    wide = states.astype(F32)
    factor = lax.rsqrt(jnp.mean(wide * wide, axis=-1, keepdims=True) + EPS)
    return wide * factor * gain


def tile_of(width, most):
    tile = min(width, most)
    while width % tile:
        tile //= 2
    return tile


def flipped(index, mask):
    out, bit = index, 1
    while bit <= mask:
        if mask & bit:
            out = out + bit * (1 - 2 * ((index // bit) % 2))
        bit *= 2
    return out


def peers_of(index, count):
    if count & (count - 1):
        return [lax.rem(index + k, count) for k in range(1, count)]
    order = sorted(range(1, count), key=lambda k: (-(k.bit_length()), k))
    return [flipped(index, k) for k in order]


def kernel(
    n,
    cores,
    tokens_ref,
    enc_gain_ref,
    final_gain_ref,
    dec_gain_ref,
    answers_ref,
    own_answers_ref,
    lengths_ref,
    owner_ref,
    rows_ref,
    w_in_hbm,
    w_out_hbm,
    w_kv_hbm,
    w_query_hbm,
    w_proj_hbm,
    encoded_ref,
    answer_ref,
    w_in,
    w_out,
    kv_pairs,
    w_kv,
    w_query,
    w_proj,
    normed_all,
    hidden,
    part,
    send1,
    recv1,
    memory_all,
    keys,
    values,
    query,
    context,
    pre_send,
    pre_recv,
    part2,
    send2,
    recv2,
    final_all,
    load_sem,
    ag_send,
    ag_recv,
    rs_send,
    rs_recv,
    mem_send,
    mem_recv,
    fwd_send,
    fwd_recv,
    pre_ssem,
    pre_rsem,
    rs2_send,
    rs2_recv,
    fin_send,
    fin_recv,
):
    me = lax.axis_index("mp")
    core = lax.axis_index("psg")
    rows, width = tokens_ref.shape
    hidden_count = w_in.shape[1]
    inner = w_query.shape[1]
    answer_count = answers_ref.shape[0]
    out_count = answer_count // n
    chunks1, chunk1 = send1.shape[0], send1.shape[-1]

    first = pl.multiple_of(core * inner, inner)
    loads = [
        pltpu.make_async_copy(w_query_hbm.at[:, pl.ds(first, inner)], w_query, load_sem.at[0]),
        pltpu.make_async_copy(w_kv_hbm.at[:, :, pl.ds(first, inner)], kv_pairs, load_sem.at[3]),
        pltpu.make_async_copy(w_in_hbm, w_in, load_sem.at[1]),
        pltpu.make_async_copy(w_out_hbm, w_out, load_sem.at[2]),
        pltpu.make_async_copy(w_proj_hbm.at[pl.ds(first, inner), :], w_proj, load_sem.at[4]),
    ]
    for load in loads:
        load.start()

    barrier = pltpu.get_barrier_semaphore()
    peers = peers_of(me, n)
    pair = me + 1 - 2 * (me % 2)
    line = [2 * place + me % 2 for place in peers_of(me // 2, n // 2)]
    others = [lax.rem(core + k, cores) for k in range(1, cores)]
    for peer in peers:
        pl.semaphore_signal(barrier, inc=1, device_id={"mp": peer}, device_id_type=MESH)
    for other in others:
        pl.semaphore_signal(barrier, inc=1, device_id={"psg": other}, device_id_type=MESH)
    normed_all[me] = norm_rows(tokens_ref[...], enc_gain_ref[...]).astype(BF16)
    pl.semaphore_wait(barrier, n - 1 + cores - 1)

    def to_peer(src, dst, send_sem, recv_sem, peer):
        return pltpu.make_async_remote_copy(
            src_ref=src, dst_ref=dst, send_sem=send_sem, recv_sem=recv_sem,
            device_id={"mp": peer}, device_id_type=MESH,
        )

    def to_core(src, dst, send_sem, recv_sem, other):
        return pltpu.make_async_remote_copy(
            src_ref=src, dst_ref=dst, send_sem=send_sem, recv_sem=recv_sem,
            device_id={"psg": other}, device_id_type=MESH,
        )

    def gather_copy(source, slot, peer):
        return to_peer(normed_all.at[source], normed_all.at[source], ag_send.at[slot], ag_recv.at[source], peer)

    for peer in line:
        gather_copy(me, peer, peer).start()
    gather_copy(me, pair, pair).start()

    normed_answer = norm_rows(answers_ref[...], dec_gain_ref[...]).astype(BF16)
    loads[0].wait()
    q_tile = tile_of(inner, 512)

    def query_step(i, carry):
        at = pl.ds(pl.multiple_of(i * q_tile, q_tile), q_tile)
        query[:, at] = jnp.dot(normed_answer, w_query[:, at], preferred_element_type=F32).astype(BF16)
        return carry

    lax.fori_loop(0, inner // q_tile, query_step, 0)

    split = tile_of(width, 64)
    half_way = width // split // 2

    def split_step(i, carry):
        at = pl.ds(pl.multiple_of(i * split, split), split)
        pairs = kv_pairs[at]
        w_kv[0, at, :] = pairs[:, 0, :]
        w_kv[1, at, :] = pairs[:, 1, :]
        return carry

    loads[1].wait()
    lax.fori_loop(0, half_way, split_step, 0)

    for peer in line[::-1]:
        gather_copy(peer, peer, peer).wait_recv()
        gather_copy(peer, peer + 1 - 2 * (me % 2), pair).start()
    loads[2].wait()
    gather_copy(pair, pair, pair).wait_recv()
    for peer in line[::-1]:
        across = peer + 1 - 2 * (me % 2)
        gather_copy(across, across, pair).wait_recv()
    for peer in line:
        gather_copy(me, peer, peer).wait_send()
        gather_copy(peer, peer + 1 - 2 * (me % 2), pair).wait_send()
    gather_copy(me, pair, pair).wait_send()

    normed = normed_all[...].reshape(n * rows, width)
    h_tile = tile_of(hidden_count, 512)

    def hidden_step(i, carry):
        at = pl.ds(pl.multiple_of(i * h_tile, h_tile), h_tile)
        product = jnp.dot(normed, w_in[:, at], preferred_element_type=F32)
        hidden[:, at] = jnp.maximum(product, 0.0).astype(BF16)
        return carry

    lax.fori_loop(0, hidden_count // h_tile, hidden_step, 0)
    loads[3].wait()

    def sum_copy(c, source, k, peer):
        return to_peer(
            send1.at[c, peer], recv1.at[c, source], rs_send.at[c, k], rs_recv.at[c, source], peer
        )

    def out_step(c, carry):
        at = pl.ds(pl.multiple_of(c * chunk1, chunk1), chunk1)
        product = jnp.dot(hidden[...], w_out[:, at], preferred_element_type=F32)
        product = product.reshape(n, rows, chunk1)
        part[c] = product
        send1[c] = product.astype(BF16)
        for k, peer in enumerate(peers):
            sum_copy(c, me, k, peer).start()
        return carry

    lax.fori_loop(0, chunks1, out_step, 0)

    lax.fori_loop(half_way, width // split, split_step, 0)

    for c in range(chunks1):
        at = slice(c * chunk1, (c + 1) * chunk1)
        total = part[c, me]
        for k, peer in enumerate(peers):
            sum_copy(c, peer, k, peer).wait_recv()
            total = total + recv1[c, peer].astype(F32)
        encoded_ref[:, at] = (tokens_ref[:, at].astype(F32) + total).astype(BF16)
    memory_all[0, me] = norm_rows(encoded_ref[...], final_gain_ref[...]).astype(BF16)

    def memory_copy(source, slot, peer):
        return to_peer(
            memory_all.at[0, source], memory_all.at[0, source], mem_send.at[slot], mem_recv.at[source], peer
        )

    def forward_copy(source, s, other):
        return to_core(
            memory_all.at[0, source], memory_all.at[cores - s, source],
            fwd_send.at[s - 1, source], fwd_recv.at[cores - s - 1, source], other,
        )

    for peer in line:
        memory_copy(me, peer, peer).start()
    memory_copy(me, pair, pair).start()
    for s, other in enumerate(others, 1):
        forward_copy(me, s, other).start()
    for c in range(chunks1):
        for k, peer in enumerate(peers):
            sum_copy(c, me, k, peer).wait_send()
    loads[4].wait()

    half = n * rows
    count = cores * half
    place_at = lax.broadcasted_iota(jnp.int32, (1, count), 1)
    slot = place_at // half
    block = (place_at % half) // rows
    token = (block * cores + (core + slot) % cores) * rows + place_at % rows
    passage = token // P_SLOT
    token_length = jnp.zeros((1, count), jnp.int32)
    token_owner = jnp.zeros((1, count), jnp.int32)
    for i in range(lengths_ref.shape[0]):
        token_length = jnp.where(passage == i, lengths_ref[i], token_length)
        token_owner = jnp.where(passage == i, owner_ref[i], token_owner)
    answer_at = lax.broadcasted_iota(jnp.int32, (answer_count, 1), 0)
    question = jnp.zeros((answer_count, 1), jnp.int32)
    end = jnp.int32(0)
    for i in range(rows_ref.shape[0]):
        end = end + rows_ref[i]
        question = question + jnp.where(answer_at >= end, 1, 0)
    token_key = jnp.where(token % P_SLOT < token_length, token_owner, -1)
    allowed = token_key == question

    for peer in line[::-1]:
        memory_copy(peer, peer, peer).wait_recv()
        memory_copy(peer, peer + 1 - 2 * (me % 2), pair).start()
        for s, other in enumerate(others, 1):
            forward_copy(peer, s, other).start()
    for peer in [me] + line[::-1]:
        across = peer + 1 - 2 * (me % 2)
        memory_copy(across, across, pair).wait_recv()
        for s, other in enumerate(others, 1):
            forward_copy(across, s, other).start()

    k_tile = tile_of(inner, 512)

    def project(s):
        memory = memory_all[s].reshape(half, width)

        def step(i, carry):
            at = pl.ds(pl.multiple_of(i * k_tile, k_tile), k_tile)
            keys[s, :, at] = jnp.dot(memory, w_kv[0, :, at], preferred_element_type=F32).astype(BF16)
            values[s, :, at] = jnp.dot(memory, w_kv[1, :, at], preferred_element_type=F32).astype(BF16)
            return carry

        lax.fori_loop(0, inner // k_tile, step, 0)

    project(0)
    for s, other in enumerate(others, 1):
        for source in [me] + peers:
            pltpu.make_async_remote_copy(
                src_ref=memory_all.at[0, source], dst_ref=memory_all.at[s, source],
                send_sem=fwd_send.at[s - 1, source], recv_sem=fwd_recv.at[s - 1, source],
                device_id={"psg": other}, device_id_type=MESH,
            ).wait_recv()
        project(s)

    for h in range(inner // DH):
        at = slice(h * DH, (h + 1) * DH)
        head_keys = keys[:, :, at].reshape(count, DH)
        head_values = values[:, :, at].reshape(count, DH)
        scores = lax.dot_general(
            query[:, at], head_keys, (((1,), (1,)), ((), ())), preferred_element_type=F32
        ) * DH ** (-0.5)
        scores = jnp.where(allowed, scores, -1e30)
        top = jnp.max(scores, axis=1, keepdims=True)
        weights = jnp.where(allowed, jnp.exp(scores - top), 0.0)
        total = jnp.sum(weights, axis=1, keepdims=True)
        summed = jnp.dot(weights.astype(BF16), head_values, preferred_element_type=F32)
        context[:, at] = (summed / total).astype(BF16)

    cut = width // cores

    def columns_of(which):
        return pl.ds(pl.multiple_of(which * cut, cut), cut)

    def project_out(which):
        return jnp.dot(context[...], w_proj[:, columns_of(which)], preferred_element_type=F32)

    def core_copy(s, other):
        return to_core(
            pre_send.at[s - 1], pre_recv.at[cores - s - 1], pre_ssem.at[s - 1], pre_rsem.at[cores - s - 1], other
        )

    for s, other in enumerate(others, 1):
        pre_send[s - 1] = project_out(other).astype(BF16)
        core_copy(s, other).start()
    product = project_out(core)
    for s, other in enumerate(others, 1):
        pltpu.make_async_remote_copy(
            src_ref=pre_send.at[s - 1], dst_ref=pre_recv.at[s - 1],
            send_sem=pre_ssem.at[s - 1], recv_sem=pre_rsem.at[s - 1],
            device_id={"psg": other}, device_id_type=MESH,
        ).wait_recv()
        product = product + pre_recv[s - 1].astype(F32)
    for j in range(n):
        block_rows = product[j * out_count : (j + 1) * out_count]
        part2[j] = block_rows
        send2[j] = block_rows.astype(BF16)

    def sum2_copy(source, k, peer):
        return to_peer(send2.at[peer], recv2.at[source], rs2_send.at[k], rs2_recv.at[source], peer)

    for k, peer in enumerate(peers):
        sum2_copy(me, k, peer).start()

    for peer in line:
        memory_copy(me, peer, peer).wait_send()
        memory_copy(peer, peer + 1 - 2 * (me % 2), pair).wait_send()
    memory_copy(me, pair, pair).wait_send()
    for s, other in enumerate(others, 1):
        for source in [me] + peers:
            forward_copy(source, s, other).wait_send()

    total = part2[me]
    for k, peer in list(enumerate(peers))[::-1]:
        sum2_copy(peer, k, peer).wait_recv()
        total = total + recv2[peer].astype(F32)
    mine = columns_of(core)
    final_all[0] = (own_answers_ref[me, :, mine].astype(F32) + total).astype(BF16)

    def final_copy(s, other):
        return to_core(
            final_all.at[0], final_all.at[cores - s], fin_send.at[s - 1], fin_recv.at[cores - s - 1], other
        )

    for s, other in enumerate(others, 1):
        final_copy(s, other).start()
    answer_ref[:, mine] = final_all[0]
    for k, peer in enumerate(peers):
        sum2_copy(me, k, peer).wait_send()
    for s, other in enumerate(others, 1):
        core_copy(s, other).wait_send()
        pltpu.make_async_remote_copy(
            src_ref=final_all.at[0], dst_ref=final_all.at[s],
            send_sem=fin_send.at[s - 1], recv_sem=fin_recv.at[s - 1],
            device_id={"psg": other}, device_id_type=MESH,
        ).wait_recv()
        answer_ref[:, columns_of(other)] = final_all[s]
    for s, other in enumerate(others, 1):
        final_copy(s, other).wait_send()


def hand_over(encoded_in, answer_in, encoded_ref, answer_ref):
    encoded_ref[...] = encoded_in[...]
    answer_ref[...] = answer_in[...]


def per_device(
    n,
    cores,
    tokens,
    enc_gain,
    w_in,
    w_out,
    final_gain,
    w_keyval,
    answer_states,
    dec_gain,
    w_query,
    w_attn_out,
    passage_lengths,
    passage_owner,
    answer_lengths,
):
    rows, width = tokens.shape
    hidden_count = w_in.shape[1]
    inner = w_query.shape[1] // cores
    answer_count = answer_states.shape[0]
    out_count = answer_count // n
    half = n * rows
    chunk1 = tile_of(width, 256)
    chunks1 = width // chunk1
    cut = width // cores
    vmem = pl.BlockSpec(memory_space=pltpu.VMEM)
    smem = pl.BlockSpec(memory_space=pltpu.SMEM)
    hbm = pl.BlockSpec(memory_space=pl.ANY)
    dma = pltpu.SemaphoreType.DMA
    others = max(cores - 1, 1)
    encoded, answer = pl.pallas_call(
        functools.partial(kernel, n, cores),
        out_shape=(
            jax.ShapeDtypeStruct((rows, width), BF16),
            jax.ShapeDtypeStruct((out_count, width), BF16),
        ),
        in_specs=[vmem] * 6 + [smem] * 3 + [hbm] * 5,
        out_specs=(vmem, vmem),
        scratch_shapes=[
            pltpu.VMEM((width, hidden_count), BF16),
            pltpu.VMEM((hidden_count, width), BF16),
            pltpu.VMEM((width, 2, inner), BF16),
            pltpu.VMEM((2, width, inner), BF16),
            pltpu.VMEM((width, inner), BF16),
            pltpu.VMEM((inner, width), BF16),
            pltpu.VMEM((n, rows, width), BF16),
            pltpu.VMEM((half, hidden_count), BF16),
            pltpu.VMEM((chunks1, n, rows, chunk1), F32),
            pltpu.VMEM((chunks1, n, rows, chunk1), BF16),
            pltpu.VMEM((chunks1, n, rows, chunk1), BF16),
            pltpu.VMEM((cores, n, rows, width), BF16),
            pltpu.VMEM((cores, half, inner), BF16),
            pltpu.VMEM((cores, half, inner), BF16),
            pltpu.VMEM((answer_count, inner), BF16),
            pltpu.VMEM((answer_count, inner), BF16),
            pltpu.VMEM((others, answer_count, cut), BF16),
            pltpu.VMEM((others, answer_count, cut), BF16),
            pltpu.VMEM((n, out_count, cut), F32),
            pltpu.VMEM((n, out_count, cut), BF16),
            pltpu.VMEM((n, out_count, cut), BF16),
            pltpu.VMEM((cores, out_count, cut), BF16),
            dma((5,)),
            dma((n,)),
            dma((n,)),
            dma((chunks1, n)),
            dma((chunks1, n)),
            dma((n,)),
            dma((n,)),
            dma((others, n)),
            dma((others, n)),
            dma((others,)),
            dma((others,)),
            dma((n,)),
            dma((n,)),
            dma((others,)),
            dma((others,)),
        ],
        compiler_params=pltpu.CompilerParams(
            collective_id=0, has_side_effects=True, vmem_limit_bytes=58 * 1024 * 1024
        ),
    )(
        tokens,
        enc_gain.reshape(1, width),
        final_gain.reshape(1, width),
        dec_gain.reshape(1, width),
        answer_states,
        answer_states.reshape(n, out_count, width),
        passage_lengths,
        passage_owner,
        answer_lengths,
        w_in,
        w_out,
        w_keyval,
        w_query,
        w_attn_out,
    )
    return pl.pallas_call(
        hand_over,
        out_shape=(
            jax.ShapeDtypeStruct(encoded.shape, BF16),
            jax.ShapeDtypeStruct(answer.shape, BF16),
        ),
        in_specs=[vmem, vmem],
        out_specs=(vmem, vmem),
    )(encoded, answer)


def solution(mesh):
    placed = (
        P(("groups", "mp", "psg"), None),
        P(),
        P(None, "mp"),
        P("mp", None),
        P(),
        P(None, None, "mp"),
        P("groups", None),
        P(),
        P(None, "mp"),
        P("mp", None),
        P("groups"),
        P("groups"),
        P("groups"),
    )
    return jax.shard_map(
        functools.partial(per_device, mesh.shape["mp"], mesh.shape["psg"]),
        mesh=mesh,
        in_specs=placed,
        out_specs=(P(("groups", "mp", "psg"), None), P(("groups", "mp"), None)),
        check_vma=False,
    )
```

```python
import functools

import jax
import jax.numpy as jnp
from jax import lax
from jax.experimental import pallas as pl
from jax.experimental.pallas import tpu as pltpu
from jax.sharding import PartitionSpec as P

DH = 128
P_SLOT = 16
EPS = 1e-06
MESH = pl.DeviceIdType.MESH
F32 = jnp.float32
BF16 = jnp.bfloat16


def norm_rows(states, gain):
    wide = states.astype(F32)
    factor = lax.rsqrt(jnp.mean(wide * wide, axis=-1, keepdims=True) + EPS)
    return wide * factor * gain


def tile_of(width, most):
    tile = min(width, most)
    while width % tile:
        tile //= 2
    return tile


def flipped(index, mask):
    out, bit = index, 1
    while bit <= mask:
        if mask & bit:
            out = out + bit * (1 - 2 * ((index // bit) % 2))
        bit *= 2
    return out


def peers_of(index, count):
    if count & (count - 1):
        return [lax.rem(index + k, count) for k in range(1, count)]
    order = sorted(range(1, count), key=lambda k: (-(k.bit_length()), k))
    return [flipped(index, k) for k in order]


def kernel(
    n,
    cores,
    tokens_ref,
    enc_gain_ref,
    final_gain_ref,
    dec_gain_ref,
    answers_ref,
    own_answers_ref,
    lengths_ref,
    owner_ref,
    rows_ref,
    w_in_hbm,
    w_out_hbm,
    w_kv_hbm,
    w_query_hbm,
    w_proj_hbm,
    encoded_ref,
    answer_ref,
    w_in,
    w_out,
    kv_pairs,
    w_kv,
    w_query,
    w_proj,
    normed_all,
    hidden,
    part,
    send1,
    recv1,
    memory_all,
    keys,
    values,
    query,
    context,
    part2,
    send2,
    recv2,
    final_all,
    load_sem,
    ag_send,
    ag_recv,
    rs_send,
    rs_recv,
    mem_send,
    mem_recv,
    fwd_send,
    fwd_recv,
    rs2_send,
    rs2_recv,
    fin_send,
    fin_recv,
):
    me = lax.axis_index("mp")
    core = lax.axis_index("psg")
    rows, width = tokens_ref.shape
    hidden_count = w_in.shape[1]
    inner = w_query.shape[1]
    answer_count = answers_ref.shape[0]
    out_count = answer_count // n
    chunks1, chunks2 = send1.shape[0], send2.shape[0]
    chunk1, chunk2 = send1.shape[-1], send2.shape[-1]

    first = pl.multiple_of(core * inner, inner)
    loads = [
        pltpu.make_async_copy(w_query_hbm.at[:, pl.ds(first, inner)], w_query, load_sem.at[0]),
        pltpu.make_async_copy(w_kv_hbm.at[:, :, pl.ds(first, inner)], kv_pairs, load_sem.at[3]),
        pltpu.make_async_copy(w_in_hbm, w_in, load_sem.at[1]),
        pltpu.make_async_copy(w_out_hbm, w_out, load_sem.at[2]),
        pltpu.make_async_copy(w_proj_hbm.at[pl.ds(first, inner), :], w_proj, load_sem.at[4]),
    ]
    for load in loads:
        load.start()

    barrier = pltpu.get_barrier_semaphore()
    peers = peers_of(me, n)
    others = [lax.rem(core + k, cores) for k in range(1, cores)]
    for peer in peers:
        pl.semaphore_signal(barrier, inc=1, device_id={"mp": peer}, device_id_type=MESH)
    for other in others:
        pl.semaphore_signal(barrier, inc=1, device_id={"psg": other}, device_id_type=MESH)
    normed_all[me] = norm_rows(tokens_ref[...], enc_gain_ref[...]).astype(BF16)
    pl.semaphore_wait(barrier, n - 1 + cores - 1)

    def to_peer(src, dst, send_sem, recv_sem, peer):
        return pltpu.make_async_remote_copy(
            src_ref=src, dst_ref=dst, send_sem=send_sem, recv_sem=recv_sem,
            device_id={"mp": peer}, device_id_type=MESH,
        )

    def to_core(src, dst, send_sem, recv_sem, other):
        return pltpu.make_async_remote_copy(
            src_ref=src, dst_ref=dst, send_sem=send_sem, recv_sem=recv_sem,
            device_id={"psg": other}, device_id_type=MESH,
        )

    def gather_copy(source, k, peer):
        return to_peer(normed_all.at[source], normed_all.at[source], ag_send.at[k], ag_recv.at[source], peer)

    for k, peer in enumerate(peers):
        gather_copy(me, k, peer).start()

    normed_answer = norm_rows(answers_ref[...], dec_gain_ref[...]).astype(BF16)
    loads[0].wait()
    q_tile = tile_of(inner, 512)

    def query_step(i, carry):
        at = pl.ds(pl.multiple_of(i * q_tile, q_tile), q_tile)
        query[:, at] = jnp.dot(normed_answer, w_query[:, at], preferred_element_type=F32).astype(BF16)
        return carry

    lax.fori_loop(0, inner // q_tile, query_step, 0)

    split = tile_of(width, 64)
    half_way = width // split // 2

    def split_step(i, carry):
        at = pl.ds(pl.multiple_of(i * split, split), split)
        pairs = kv_pairs[at]
        w_kv[0, at, :] = pairs[:, 0, :]
        w_kv[1, at, :] = pairs[:, 1, :]
        return carry

    loads[1].wait()
    lax.fori_loop(0, half_way, split_step, 0)

    loads[2].wait()
    for k, peer in enumerate(peers):
        gather_copy(peer, k, peer).wait_recv()
    for k, peer in enumerate(peers):
        gather_copy(me, k, peer).wait_send()

    normed = normed_all[...].reshape(n * rows, width)
    h_tile = tile_of(hidden_count, 512)

    def hidden_step(i, carry):
        at = pl.ds(pl.multiple_of(i * h_tile, h_tile), h_tile)
        product = jnp.dot(normed, w_in[:, at], preferred_element_type=F32)
        hidden[:, at] = jnp.maximum(product, 0.0).astype(BF16)
        return carry

    lax.fori_loop(0, hidden_count // h_tile, hidden_step, 0)
    loads[3].wait()

    def sum_copy(c, source, k, peer):
        return to_peer(
            send1.at[c, peer], recv1.at[c, source], rs_send.at[c, k], rs_recv.at[c, source], peer
        )

    def out_step(c, carry):
        at = pl.ds(pl.multiple_of(c * chunk1, chunk1), chunk1)
        product = jnp.dot(hidden[...], w_out[:, at], preferred_element_type=F32)
        product = product.reshape(n, rows, chunk1)
        part[c] = product
        send1[c] = product.astype(BF16)
        for k, peer in enumerate(peers):
            sum_copy(c, me, k, peer).start()
        return carry

    lax.fori_loop(0, chunks1, out_step, 0)

    lax.fori_loop(half_way, width // split, split_step, 0)

    for c in range(chunks1):
        at = slice(c * chunk1, (c + 1) * chunk1)
        total = part[c, me]
        for k, peer in enumerate(peers):
            sum_copy(c, peer, k, peer).wait_recv()
            total = total + recv1[c, peer].astype(F32)
        encoded_ref[:, at] = (tokens_ref[:, at].astype(F32) + total).astype(BF16)
    memory_all[0, me] = norm_rows(encoded_ref[...], final_gain_ref[...]).astype(BF16)

    def memory_copy(source, k, peer):
        return to_peer(
            memory_all.at[0, source], memory_all.at[0, source], mem_send.at[k], mem_recv.at[source], peer
        )

    def forward_copy(source, s, other):
        return to_core(
            memory_all.at[0, source], memory_all.at[cores - s, source],
            fwd_send.at[s - 1, source], fwd_recv.at[cores - s - 1, source], other,
        )

    for k, peer in enumerate(peers):
        memory_copy(me, k, peer).start()
    for s, other in enumerate(others, 1):
        forward_copy(me, s, other).start()
    for c in range(chunks1):
        for k, peer in enumerate(peers):
            sum_copy(c, me, k, peer).wait_send()
    loads[4].wait()

    half = n * rows
    count = cores * half
    place_at = lax.broadcasted_iota(jnp.int32, (1, count), 1)
    slot = place_at // half
    block = (place_at % half) // rows
    token = (block * cores + (core + slot) % cores) * rows + place_at % rows
    passage = token // P_SLOT
    token_length = jnp.zeros((1, count), jnp.int32)
    token_owner = jnp.zeros((1, count), jnp.int32)
    for i in range(lengths_ref.shape[0]):
        token_length = jnp.where(passage == i, lengths_ref[i], token_length)
        token_owner = jnp.where(passage == i, owner_ref[i], token_owner)
    answer_at = lax.broadcasted_iota(jnp.int32, (answer_count, 1), 0)
    question = jnp.zeros((answer_count, 1), jnp.int32)
    end = jnp.int32(0)
    for i in range(rows_ref.shape[0]):
        end = end + rows_ref[i]
        question = question + jnp.where(answer_at >= end, 1, 0)
    token_key = jnp.where(token % P_SLOT < token_length, token_owner, -1)
    allowed = token_key == question

    for k, peer in enumerate(peers):
        memory_copy(peer, k, peer).wait_recv()
        for s, other in enumerate(others, 1):
            forward_copy(peer, s, other).start()

    k_tile = tile_of(inner, 512)

    def project(s):
        memory = memory_all[s].reshape(half, width)

        def step(i, carry):
            at = pl.ds(pl.multiple_of(i * k_tile, k_tile), k_tile)
            keys[s, :, at] = jnp.dot(memory, w_kv[0, :, at], preferred_element_type=F32).astype(BF16)
            values[s, :, at] = jnp.dot(memory, w_kv[1, :, at], preferred_element_type=F32).astype(BF16)
            return carry

        lax.fori_loop(0, inner // k_tile, step, 0)

    project(0)
    for s, other in enumerate(others, 1):
        for source in [me] + peers:
            pltpu.make_async_remote_copy(
                src_ref=memory_all.at[0, source], dst_ref=memory_all.at[s, source],
                send_sem=fwd_send.at[s - 1, source], recv_sem=fwd_recv.at[s - 1, source],
                device_id={"psg": other}, device_id_type=MESH,
            ).wait_recv()
        project(s)

    for h in range(inner // DH):
        at = slice(h * DH, (h + 1) * DH)
        head_keys = keys[:, :, at].reshape(count, DH)
        head_values = values[:, :, at].reshape(count, DH)
        scores = lax.dot_general(
            query[:, at], head_keys, (((1,), (1,)), ((), ())), preferred_element_type=F32
        ) * DH ** (-0.5)
        scores = jnp.where(allowed, scores, -1e30)
        top = jnp.max(scores, axis=1, keepdims=True)
        weights = jnp.where(allowed, jnp.exp(scores - top), 0.0)
        total = jnp.sum(weights, axis=1, keepdims=True)
        summed = jnp.dot(weights.astype(BF16), head_values, preferred_element_type=F32)
        context[:, at] = (summed / total).astype(BF16)

    def sum2_copy(c, source, k, peer):
        return to_peer(
            send2.at[c, peer], recv2.at[c, source], rs2_send.at[c, k], rs2_recv.at[c, source], peer
        )

    for c in range(chunks2):
        product = jnp.dot(
            context[...], w_proj[:, c * chunk2 : (c + 1) * chunk2], preferred_element_type=F32
        )
        for j in range(n):
            block_rows = product[j * out_count : (j + 1) * out_count]
            part2[c, j] = block_rows
            send2[c, j] = block_rows.astype(BF16)
        for k, peer in enumerate(peers):
            sum2_copy(c, me, k, peer).start()

    for k, peer in enumerate(peers):
        memory_copy(me, k, peer).wait_send()
    for s, other in enumerate(others, 1):
        for source in [me] + peers:
            forward_copy(source, s, other).wait_send()

    for c in range(chunks2):
        total = part2[c, me]
        for k, peer in enumerate(peers):
            sum2_copy(c, peer, k, peer).wait_recv()
            total = total + recv2[c, peer].astype(F32)
        final_all[0, :, c * chunk2 : (c + 1) * chunk2] = total

    def final_copy(s, other):
        return to_core(
            final_all.at[0], final_all.at[cores - s], fin_send.at[s - 1], fin_recv.at[cores - s - 1], other
        )

    for s, other in enumerate(others, 1):
        final_copy(s, other).start()
    for c in range(chunks2):
        for k, peer in enumerate(peers):
            sum2_copy(c, me, k, peer).wait_send()
    total = final_all[0]
    for s, other in enumerate(others, 1):
        pltpu.make_async_remote_copy(
            src_ref=final_all.at[0], dst_ref=final_all.at[s],
            send_sem=fin_send.at[s - 1], recv_sem=fin_recv.at[s - 1],
            device_id={"psg": other}, device_id_type=MESH,
        ).wait_recv()
        total = total + final_all[s]
    answer_ref[...] = (own_answers_ref[me].astype(F32) + total).astype(BF16)
    for s, other in enumerate(others, 1):
        final_copy(s, other).wait_send()


def hand_over(encoded_in, answer_in, encoded_ref, answer_ref):
    encoded_ref[...] = encoded_in[...]
    answer_ref[...] = answer_in[...]


def per_device(
    n,
    cores,
    tokens,
    enc_gain,
    w_in,
    w_out,
    final_gain,
    w_keyval,
    answer_states,
    dec_gain,
    w_query,
    w_attn_out,
    passage_lengths,
    passage_owner,
    answer_lengths,
):
    rows, width = tokens.shape
    hidden_count = w_in.shape[1]
    inner = w_query.shape[1] // cores
    answer_count = answer_states.shape[0]
    out_count = answer_count // n
    half = n * rows
    chunk1 = tile_of(width, 512)
    chunk2 = tile_of(width, 512)
    chunks1, chunks2 = width // chunk1, width // chunk2
    vmem = pl.BlockSpec(memory_space=pltpu.VMEM)
    smem = pl.BlockSpec(memory_space=pltpu.SMEM)
    hbm = pl.BlockSpec(memory_space=pl.ANY)
    dma = pltpu.SemaphoreType.DMA
    others = max(cores - 1, 1)
    encoded, answer = pl.pallas_call(
        functools.partial(kernel, n, cores),
        out_shape=(
            jax.ShapeDtypeStruct((rows, width), BF16),
            jax.ShapeDtypeStruct((out_count, width), BF16),
        ),
        in_specs=[vmem] * 6 + [smem] * 3 + [hbm] * 5,
        out_specs=(vmem, vmem),
        scratch_shapes=[
            pltpu.VMEM((width, hidden_count), BF16),
            pltpu.VMEM((hidden_count, width), BF16),
            pltpu.VMEM((width, 2, inner), BF16),
            pltpu.VMEM((2, width, inner), BF16),
            pltpu.VMEM((width, inner), BF16),
            pltpu.VMEM((inner, width), BF16),
            pltpu.VMEM((n, rows, width), BF16),
            pltpu.VMEM((half, hidden_count), BF16),
            pltpu.VMEM((chunks1, n, rows, chunk1), F32),
            pltpu.VMEM((chunks1, n, rows, chunk1), BF16),
            pltpu.VMEM((chunks1, n, rows, chunk1), BF16),
            pltpu.VMEM((cores, n, rows, width), BF16),
            pltpu.VMEM((cores, half, inner), BF16),
            pltpu.VMEM((cores, half, inner), BF16),
            pltpu.VMEM((answer_count, inner), BF16),
            pltpu.VMEM((answer_count, inner), BF16),
            pltpu.VMEM((chunks2, n, out_count, chunk2), F32),
            pltpu.VMEM((chunks2, n, out_count, chunk2), BF16),
            pltpu.VMEM((chunks2, n, out_count, chunk2), BF16),
            pltpu.VMEM((cores, out_count, width), F32),
            dma((5,)),
            dma((n,)),
            dma((n,)),
            dma((chunks1, n)),
            dma((chunks1, n)),
            dma((n,)),
            dma((n,)),
            dma((others, n)),
            dma((others, n)),
            dma((chunks2, n)),
            dma((chunks2, n)),
            dma((others,)),
            dma((others,)),
        ],
        compiler_params=pltpu.CompilerParams(
            collective_id=0, has_side_effects=True, vmem_limit_bytes=58 * 1024 * 1024
        ),
    )(
        tokens,
        enc_gain.reshape(1, width),
        final_gain.reshape(1, width),
        dec_gain.reshape(1, width),
        answer_states,
        answer_states.reshape(n, out_count, width),
        passage_lengths,
        passage_owner,
        answer_lengths,
        w_in,
        w_out,
        w_keyval,
        w_query,
        w_attn_out,
    )
    return pl.pallas_call(
        hand_over,
        out_shape=(
            jax.ShapeDtypeStruct(encoded.shape, BF16),
            jax.ShapeDtypeStruct(answer.shape, BF16),
        ),
        in_specs=[vmem, vmem],
        out_specs=(vmem, vmem),
    )(encoded, answer)


def solution(mesh):
    placed = (
        P(("groups", "mp", "psg"), None),
        P(),
        P(None, "mp"),
        P("mp", None),
        P(),
        P(None, None, "mp"),
        P("groups", None),
        P(),
        P(None, "mp"),
        P("mp", None),
        P("groups"),
        P("groups"),
        P("groups"),
    )
    return jax.shard_map(
        functools.partial(per_device, mesh.shape["mp"], mesh.shape["psg"]),
        mesh=mesh,
        in_specs=placed,
        out_specs=(P(("groups", "mp", "psg"), None), P(("groups", "mp"), None)),
        check_vma=False,
    )
```
